32 devices in a mesh: comp: 4 (over z), tile: 8 (over y, x, core).
Axes of the slice: x: 2, y: 2, z: 4, core: 2. Of those that a mesh axis runs over, the one named last changes fastest.
Arguments:
- coupled_state: float32 [4, 640, 48, 128], P('comp', None, 'tile'), may hold values from -6 to 6
- diffusivity: float32 [4, 640], P('comp'), may hold values from 0.02 to 0.24
- coupling: bfloat16 [4, 4, 640, 640], P('comp'), may hold values from -0.25 to 0.25
- regrid_weights: bfloat16 [4, 8, 6, 768, 768], P('comp', 'tile'), may hold values from -0.09375 to 0.09375
- source_offsets: int32 [4, 8, 6], P('comp', 'tile'), may hold values from -3 to 3, as said below
- sea_mask: int32 [4, 48, 128], P('comp', 'tile'), may hold values 0 or 1
Outputs:
- coupled_next: float32 [4, 640, 48, 128], P('comp', None, 'tile')
The draws below stay inside these ranges and needn't reach their ends.
Inputs may be any that keep to these rules, and one draw needn't show every extreme that they name: `source_offsets`: the 6 offsets of one target tile are distinct.
All inputs are finite; a program needn't handle non-finite values. No bound on the sum of `sea_mask` on one device may be relied on, other than what follows from the above.
Results may differ from the reference program's by a relative error of at most 0.0042.
Values may be sent and summed in bfloat16 or wider, within the bound.
A program may use at most 192 MiB of HBM per device.

```python
import math
import jax
import jax.numpy as jnp
from jax import lax

CH = 640
COLS = 128
SWEEPS = 4
PAIRS = 6
REACH = 3
SLOTS = 4
NTILES = 8
CELLS = 768
GROWS = 48


def pick_offsets(one_key):
    return jax.random.permutation(one_key, 2 * REACH + 1)[:PAIRS]


def draw_source_offsets(key, part):
    row_keys = jax.random.split(jax.random.fold_in(key, 17), SLOTS * NTILES)
    chosen = jax.vmap(pick_offsets)(row_keys)
    return chosen.reshape(SLOTS, NTILES, PAIRS).astype(jnp.int32) - REACH


def with_ends(result, stream_key, smallest, largest):
    extent = result.shape
    index_at = [jax.random.randint(jax.random.fold_in(stream_key, axis), (), 0, extent[axis]) for axis in range(len(extent))]
    result = result.at[tuple(index_at)].set(smallest)
    longest = extent.index(max(extent))
    index_at[longest] = (index_at[longest] + 1) % extent[longest]
    return result.at[tuple(index_at)].set(largest)


def block_scale(own_key, shape, cuts, smallest, top_value):
    factor_of = 1.0
    for position, blocks in cuts:
        steps = jax.random.uniform(jax.random.fold_in(jax.random.fold_in(own_key, 6), position), (blocks,), jnp.float32, smallest / len(cuts), top_value / len(cuts))
        factor_of = factor_of * jnp.repeat(jnp.exp(steps), shape[position] // blocks).reshape((-1,) + (1,) * (len(shape) - 1 - position))
    return factor_of


def centred(stream_key, shape, deviation, most, cuts=(), kind=jnp.bfloat16):
    factor_of = block_scale(stream_key, shape, cuts, -0.22, 0.18) if cuts else 1.0
    drawn = jax.random.normal(stream_key, shape, jnp.float32) * deviation * factor_of
    return jnp.minimum(jnp.maximum(drawn, -most), most).astype(kind)


def setup_inputs(seed: int = 0) -> dict:
    streams_of = jax.random.split(jax.random.key(seed), 7)
    return {
        "coupled_state": centred(streams_of[0], (SLOTS, CH, GROWS, COLS), 1.0, 6.0, ((0, 4), (2, 8)), jnp.float32),
        "diffusivity": jnp.clip(jnp.exp(math.log(0.24) - 2.4849066 * jax.random.uniform(streams_of[1], (SLOTS, CH), jnp.float32) ** block_scale(streams_of[1], (SLOTS, CH), ((0, 4),), -0.2, 0.2)), 0.02, 0.24),
        "coupling": centred(streams_of[2], (SLOTS, SLOTS, CH, CH), CH ** -0.5, 0.25, ((0, 4),)),
        "regrid_weights": centred(streams_of[3], (SLOTS, NTILES, PAIRS, CELLS, CELLS), (PAIRS * CELLS) ** -0.5, 0.09375, ((0, 4), (1, 8))),
        "source_offsets": draw_source_offsets(jax.random.fold_in(streams_of[6], 71), 0),
        "sea_mask": with_ends((jax.random.randint(streams_of[5], (SLOTS, GROWS, COLS), 0, 4) < 3).astype(jnp.int32), jax.random.fold_in(streams_of[5], 1), 0, 1),
    }


section_links = ((0, 0, 1, 1), (0, 0, 1, 1), (1, 1, 0, 1), (0, 0, 1, 0))


def diffuse(field_now, rate_col):
    above = jnp.roll(field_now, 1, axis=2)
    below = jnp.roll(field_now, -1, axis=2)
    beside = jnp.pad(field_now, ((0, 0), (0, 0), (0, 0), (1, 1)))
    laplacian = below + above + beside[..., 2:] + beside[..., :-2] - 4.0 * field_now
    return field_now + rate_col * laplacian


def reference(coupled_state, diffusivity, coupling, regrid_weights, source_offsets, sea_mask):
    stepped = coupled_state
    rate_col = diffusivity[:, :, None, None]
    for sweep_index in range(SWEEPS):
        stepped = diffuse(stepped, rate_col)
    lowered = coupled_state.astype(jnp.bfloat16).reshape(SLOTS, CH, NTILES * CELLS)
    tile_ids = jnp.arange(NTILES, dtype=jnp.int32)
    results = []
    for target in range(SLOTS):
        running = jnp.zeros((CH, NTILES * CELLS), jnp.float32)
        for source in range(SLOTS):
            if section_links[source][target] == 1:
                product = jnp.dot(coupling[source, target], lowered[source], preferred_element_type=jnp.float32)
                partial_term = lax.optimization_barrier(product.astype(jnp.bfloat16))
                running = running + partial_term.astype(jnp.float32)
        forcing = running.astype(jnp.bfloat16).reshape(CH, NTILES, CELLS)
        source_tiles = ((tile_ids[:, None] + source_offsets[target]) % NTILES).astype(jnp.int32)
        gathered = forcing[:, source_tiles, :].astype(jnp.float32)
        blocks = regrid_weights[target].astype(jnp.float32)
        regridded = jnp.einsum("ctkx,tkyx->cty", gathered, blocks)
        results.append(regridded.reshape(CH, GROWS, COLS))
    regridded_all = jnp.stack(results, axis=0)
    return jnp.where(sea_mask[:, None] == 1, stepped + regridded_all, coupled_state)
```

```python
import functools

import jax
import jax.numpy as jnp
from jax import lax
from jax.experimental import pallas as pl
from jax.experimental.pallas import tpu as pltpu
from jax.sharding import PartitionSpec as P

SWEEPS = 4
REACH = 3
CHUNK = 64
MESH = pl.DeviceIdType.MESH


def flip(index, bit):
    return index + bit - 2 * bit * lax.rem(lax.div(index, bit), 2)


def body(
    slots, tiles, chunk,
    x_ref, diff_ref, coup_ref, regw_ref, off_ref, mask_ref,
    out_ref,
    xb, rate, cbuf, wbuf, gbuf, pbuf, abuf, fbuf, halo,
    csend, crecv, hsend, hrecv, gsend, grecv, lsem,
):
    s = lax.axis_index("comp")
    t = lax.axis_index("tile")
    rows_here, channels, columns = x_ref.shape
    pairs = regw_ref.shape[0]
    edge = SWEEPS * columns
    cells = rows_here * columns
    count = channels // chunk
    half = chunk // 2
    paired = tiles == 8

    loads = [
        pltpu.make_async_copy(coup_ref.at[3 - lax.div(s, 3)], cbuf.at[0], lsem.at[0]),
        pltpu.make_async_copy(coup_ref.at[2 - 2 * lax.div(s, 2)], cbuf.at[1], lsem.at[1]),
        pltpu.make_async_copy(coup_ref.at[1], cbuf.at[2], lsem.at[2]),
        pltpu.make_async_copy(regw_ref, wbuf.at[pl.ds(0, pairs)], lsem.at[3]),
    ]
    for load in loads:
        load.start()

    barrier = pltpu.get_barrier_semaphore()
    steps = range(1, tiles) if paired else [d for r in range(1, REACH + 1) for d in (r, tiles - r)]
    greeted = [(lax.rem(s + d, slots), t) for d in range(1, slots)]
    greeted += [(s, lax.rem(t + d, tiles)) for d in steps]
    for other in greeted:
        pl.semaphore_signal(barrier, inc=1, device_id=other, device_id_type=MESH)

    for r in range(rows_here):
        xb[:, r * columns : (r + 1) * columns] = x_ref[r].astype(jnp.bfloat16)
    wbuf[pairs] = jnp.zeros_like(wbuf[pairs])
    for c in range(channels // columns):
        row = jnp.broadcast_to(diff_ref[:, c * columns : (c + 1) * columns], (columns, columns))
        rate[c * columns : (c + 1) * columns, :] = row.T

    pl.semaphore_wait(barrier, len(greeted))

    def send(src, dst, send_sem, recv_sem, where):
        return pltpu.make_async_remote_copy(
            src_ref=src, dst_ref=dst, send_sem=send_sem, recv_sem=recv_sem,
            device_id=where, device_id_type=MESH,
        )

    below = (s, lax.rem(t + 1, tiles))
    above = (s, lax.rem(t + tiles - 1, tiles))
    halos = [
        send(xb.at[:, pl.ds(cells - edge, edge)], halo.at[0], hsend.at[0], hrecv.at[0], below),
        send(xb.at[:, pl.ds(0, edge)], halo.at[1], hsend.at[1], hrecv.at[1], above),
    ]

    def span(i):
        return pl.ds(pl.multiple_of(i * chunk, chunk), chunk)

    def project(which, i):
        pbuf[which, span(i), :] = jnp.dot(
            cbuf[which, span(i), :], xb[...], preferred_element_type=jnp.float32
        ).astype(jnp.bfloat16)

    def to_a(i, where):
        return send(pbuf.at[0, span(i), :], abuf.at[0, span(i), :], csend.at[0, i], crecv.at[0, i], where)

    def to_b(i, where):
        return send(pbuf.at[1, span(i), :], abuf.at[1, span(i), :], csend.at[1, i], crecv.at[1, i], where)

    def to_f(which, i, where):
        return send(
            pbuf.at[which, span(i), :], fbuf.at[span(i), :], csend.at[which, i], crecv.at[2, i], where
        )

    up1 = (lax.rem(s + 1, slots), t)

    def out_copies(section, i):
        if section in (0, 1):
            return [to_a(i, (section + 1, t)), to_b(i, (section + 1, t))]
        if section == 2:
            return [to_f(0, i, (3, t)), to_f(1, i, (0, t)), to_f(2, i, (1, t))]
        return [to_f(0, i, (2, t))]

    near = {b: (s, flip(t, b)) for b in (1, 2, 4)} if paired else {}
    if paired:
        near[5] = (s, flip(flip(t, 4), 1))
        own = 0
        held = (1, 2, 3, 5, 6, 7)
    else:
        own = REACH
        held = tuple(o for o in range(2 * REACH + 1) if o != REACH)

    def first(i):
        return pl.ds(pl.multiple_of(i * chunk, half), half)

    def second(i):
        return pl.ds(pl.multiple_of(i * chunk + half, half), half)

    def relay(n, i, src, dst, part, where):
        return send(
            src.at[part, :], gbuf.at[dst, part, :], gsend.at[n, i], grecv.at[n, i], where
        )

    def gather1(i):
        if paired:
            return [
                relay(0, i, fbuf, 1, span(i), near[1]),
                relay(1, i, fbuf, 2, span(i), near[2]),
                relay(2, i, fbuf, 5, span(i), near[5]),
            ]
        copies = []
        for n, o in enumerate(held):
            d = REACH - o
            copies.append(relay(n, i, fbuf, o, span(i), (s, lax.rem(t + tiles + d, tiles))))
        return copies

    def gather2(i):
        if not paired:
            return []
        return [
            relay(3, i, gbuf.at[2], 3, span(i), near[1]),
            relay(4, i, gbuf.at[2], 6, first(i), near[4]),
            relay(5, i, gbuf.at[5], 7, second(i), near[2]),
        ]

    def gather3(i):
        if not paired:
            return []
        return [
            relay(6, i, gbuf.at[6], 7, first(i), near[1]),
            relay(7, i, gbuf.at[7], 6, second(i), near[1]),
        ]

    def block_of(slot):
        if paired:
            tile = t
            for bit in (1, 2, 4):
                if slot & bit:
                    tile = flip(tile, bit)
            offset = lax.rem(tile - t + tiles + REACH, tiles) - REACH
        else:
            offset = slot - REACH
        found = jnp.int32(pairs)
        for k in range(pairs):
            found = jnp.where(off_ref[0, k] == offset, jnp.int32(k), found)
        return found

    loads[0].wait()
    loads[1].wait()
    loads[2].wait()

    def phase_a(i, carry):
        @pl.when(s == 0)
        def _():
            project(0, i)
            to_a(i, (1, t)).start()
            project(1, i)
            to_b(i, (1, t)).start()

        @pl.when(s == 2)
        def _():
            project(2, i)
            to_f(2, i, (1, t)).start()
            project(1, i)
            to_f(1, i, (0, t)).start()

        @pl.when(s == 3)
        def _():
            project(0, i)
            to_f(0, i, (2, t)).start()

        return carry

    for copy in halos:
        copy.start()
    lax.fori_loop(0, count, phase_a, 0)
    loads[3].wait()
    blocks = {slot: block_of(slot) for slot in (own,) + held}

    def add_to(which, landed, i):
        pbuf[which, span(i), :] = (
            pbuf[which, span(i), :].astype(jnp.float32) + landed[span(i), :].astype(jnp.float32)
        ).astype(jnp.bfloat16)

    def forcing(i):
        @pl.when(s == 1)
        def _():
            project(0, i)
            to_a(i, (2, t)).wait_recv()
            add_to(0, abuf.at[0], i)
            to_a(i, (2, t)).start()
            project(1, i)
            to_b(i, (2, t)).wait_recv()
            add_to(1, abuf.at[1], i)
            to_b(i, (2, t)).start()

        @pl.when(s == 2)
        def _():
            project(0, i)
            to_a(i, (3, t)).wait_recv()
            add_to(0, abuf.at[0], i)
            to_f(0, i, (3, t)).start()
            to_b(i, (3, t)).wait_recv()

        to_f(0, i, up1).wait_recv()

        @pl.when(s == 2)
        def _():
            fbuf[span(i), :] = (
                fbuf[span(i), :].astype(jnp.float32) + abuf[1, span(i), :].astype(jnp.float32)
            ).astype(jnp.bfloat16)

        for copy in gather1(i):
            copy.start()

    def diffuse(i):
        lane = lax.broadcasted_iota(jnp.int32, (16, columns), 1)
        inner_low = lane > 0
        inner_high = lane < columns - 1

        def block(j, carry):
            rows = pl.ds(pl.multiple_of(i * chunk + j * 16, 16), 16)
            scale = rate[rows, :]
            planes = [
                halo[0, rows, r * columns : (r + 1) * columns].astype(jnp.float32) for r in range(SWEEPS)
            ]
            planes += [x_ref[r, rows, :] for r in range(rows_here)]
            planes += [
                halo[1, rows, r * columns : (r + 1) * columns].astype(jnp.float32) for r in range(SWEEPS)
            ]
            for _ in range(SWEEPS):
                fresh = []
                for r in range(1, len(planes) - 1):
                    mid = planes[r]
                    left = jnp.where(inner_low, pltpu.roll(mid, 1, 1), 0.0)
                    right = jnp.where(inner_high, pltpu.roll(mid, columns - 1, 1), 0.0)
                    lap = planes[r + 1] + planes[r - 1] + right + left - 4.0 * mid
                    fresh.append(mid + scale * lap)
                planes = fresh
            for r in range(rows_here):
                out_ref[r, rows, :] = planes[r]
            return carry

        lax.fori_loop(0, chunk // 16, block, 0)

    def finish(i):
        dims = (((1,), (1,)), ((), ()))
        total = lax.dot_general(
            fbuf[span(i), :], wbuf[blocks[own]], dims, preferred_element_type=jnp.float32
        )
        for slot in held:
            total += lax.dot_general(
                gbuf[slot, span(i), :], wbuf[blocks[slot]], dims, preferred_element_type=jnp.float32
            )
        for r in range(rows_here):
            here = total[:, r * columns : (r + 1) * columns]
            out_ref[r, span(i), :] = jnp.where(
                mask_ref[r] == 1, out_ref[r, span(i), :] + here, x_ref[r, span(i), :]
            )

    def phase_b(i, carry):
        @pl.when(i < count)
        def _():
            forcing(i)

        @pl.when((i >= 1) & (i < count + 1))
        def _():
            if paired:
                one = gather1(i - 1)
                two = gather2(i - 1)
                one[1].wait_recv()
                two[0].start()
                two[1].start()
                one[2].wait_recv()
                two[2].start()

        @pl.when(i == 2)
        def _():
            for copy in halos:
                copy.wait_recv()

        @pl.when((i >= 2) & (i < count + 2))
        def _():
            if paired:
                two = gather2(i - 2)
                three = gather3(i - 2)
                two[1].wait_recv()
                three[0].start()
                two[2].wait_recv()
                three[1].start()
            diffuse(i - 2)

        @pl.when(i >= 3)
        def _():
            if paired:
                gather1(i - 3)[0].wait_recv()
                gather2(i - 3)[0].wait_recv()
                for copy in gather3(i - 3):
                    copy.wait_recv()
            else:
                for copy in gather1(i - 3):
                    copy.wait_recv()
            finish(i - 3)

        return carry

    lax.fori_loop(0, count + 3, phase_b, 0)

    def drain(i, carry):
        for section in range(slots):
            @pl.when(s == section)
            def _():
                for copy in out_copies(section, i):
                    copy.wait_send()
        for copy in gather1(i) + gather2(i) + gather3(i):
            copy.wait_send()
        return carry

    lax.fori_loop(0, count, drain, 0)
    for copy in halos:
        copy.wait_send()


def shards(slots, tiles, coupled_state, diffusivity, coupling, regrid_weights, source_offsets, sea_mask):
    _, channels, rows_here, columns = coupled_state.shape
    cells = rows_here * columns
    pairs = regrid_weights.shape[2]
    chunk = CHUNK
    count = channels // chunk
    vmem = pl.BlockSpec(memory_space=pltpu.VMEM)
    smem = pl.BlockSpec(memory_space=pltpu.SMEM)
    anyspace = pl.BlockSpec(memory_space=pl.ANY)
    dma = pltpu.SemaphoreType.DMA
    low = jnp.bfloat16
    held = 8 if tiles == 8 else 2 * REACH + 1
    result = pl.pallas_call(
        functools.partial(body, slots, tiles, chunk),
        out_shape=jax.ShapeDtypeStruct((rows_here, channels, columns), jnp.float32),
        in_specs=[vmem, vmem, anyspace, anyspace, smem, vmem],
        out_specs=vmem,
        scratch_shapes=[
            pltpu.VMEM((channels, cells), low),
            pltpu.VMEM((channels, columns), jnp.float32),
            pltpu.VMEM((3, channels, channels), low),
            pltpu.VMEM((pairs + 1, cells, cells), low),
            pltpu.VMEM((held, channels, cells), low),
            pltpu.VMEM((3, channels, cells), low),
            pltpu.VMEM((2, channels, cells), low),
            pltpu.VMEM((channels, cells), low),
            pltpu.VMEM((2, channels, SWEEPS * columns), low),
            dma((3, count)),
            dma((3, count)),
            dma((2,)),
            dma((2,)),
            dma((8, count)),
            dma((8, count)),
            dma((4,)),
        ],
        compiler_params=pltpu.CompilerParams(
            collective_id=0, has_side_effects=True, vmem_limit_bytes=60 * 1024 * 1024
        ),
        name="exchange",
    )(
        coupled_state[0].transpose(1, 0, 2),
        diffusivity,
        coupling[0],
        regrid_weights[0, 0],
        source_offsets[0],
        sea_mask[0][:, None, :],
    )
    return result.transpose(1, 0, 2)[None]


def solution(mesh):
    in_specs = (
        P("comp", None, "tile", None),
        P("comp", None),
        P("comp", None, None, None),
        P("comp", "tile", None, None, None),
        P("comp", "tile", None),
        P("comp", "tile", None),
    )
    out_specs = P("comp", None, "tile", None)
    run = functools.partial(shards, mesh.shape["comp"], mesh.shape["tile"])
    return jax.shard_map(run, mesh=mesh, in_specs=in_specs, out_specs=out_specs, check_vma=False)
```

```python
import functools

import jax
import jax.numpy as jnp
from jax import lax
from jax.experimental import pallas as pl
from jax.experimental.pallas import tpu as pltpu
from jax.sharding import PartitionSpec as P

SWEEPS = 4
REACH = 3
CHUNK = 128
EXTRA = 0
MESH = pl.DeviceIdType.MESH


def flip(index, bit):
    return index + bit - 2 * bit * lax.rem(lax.div(index, bit), 2)


def body(
    slots, tiles, chunk,
    xin_ref, diff_ref, coup_ref, regw_ref, off_ref, mask_ref,
    result_ref,
    x_ref, out_ref, xb, rate, cbuf, wraw, wbuf, gbuf, pbuf, abuf, fbuf, halo,
    csend, crecv, hsend, hrecv, gsend, grecv, lsem, osem,
):
    s = lax.axis_index("comp")
    t = lax.axis_index("tile")
    rows_here, channels, columns = x_ref.shape
    pairs = regw_ref.shape[0]
    edge = SWEEPS * columns
    cells = rows_here * columns
    count = channels // chunk
    part = chunk * 5 // 8 // 8 * 8
    paired = tiles == 8

    load_x = pltpu.make_async_copy(xin_ref, x_ref, lsem.at[4])
    load_x.start()
    loads = [
        pltpu.make_async_copy(coup_ref.at[3 - lax.div(s, 3)], cbuf.at[0], lsem.at[0]),
        pltpu.make_async_copy(coup_ref.at[2 - 2 * lax.div(s, 2)], cbuf.at[1], lsem.at[1]),
        pltpu.make_async_copy(coup_ref.at[1], cbuf.at[2], lsem.at[2]),
        pltpu.make_async_copy(regw_ref, wraw, lsem.at[3]),
    ]
    for load in loads[:3]:
        load.start()

    barrier = pltpu.get_barrier_semaphore()
    steps = range(1, tiles) if paired else [d for r in range(1, REACH + 1) for d in (r, tiles - r)]
    greeted = [(lax.rem(s + d, slots), t) for d in range(1, slots)]
    greeted += [(s, lax.rem(t + d, tiles)) for d in steps]
    for other in greeted:
        pl.semaphore_signal(barrier, inc=1, device_id=other, device_id_type=MESH)

    wbuf[pairs] = jnp.zeros_like(wbuf[pairs])
    load_x.wait()
    for r in range(rows_here):
        xb[:, r * columns : (r + 1) * columns] = x_ref[r].astype(jnp.bfloat16)
    for c in range(channels // columns):
        row = jnp.broadcast_to(diff_ref[:, c * columns : (c + 1) * columns], (columns, columns))
        rate[c * columns : (c + 1) * columns, :] = row.T

    pl.semaphore_wait(barrier, len(greeted))

    def send(src, dst, send_sem, recv_sem, where):
        return pltpu.make_async_remote_copy(
            src_ref=src, dst_ref=dst, send_sem=send_sem, recv_sem=recv_sem,
            device_id=where, device_id_type=MESH,
        )

    below = (s, lax.rem(t + 1, tiles))
    above = (s, lax.rem(t + tiles - 1, tiles))
    def halos(i):
        return [
            send(
                xb.at[span(i), pl.ds(cells - edge, edge)], halo.at[0, span(i), :],
                hsend.at[0, i], hrecv.at[0, i], below,
            ),
            send(
                xb.at[span(i), pl.ds(0, edge)], halo.at[1, span(i), :],
                hsend.at[1, i], hrecv.at[1, i], above,
            ),
        ]

    def span(i):
        return pl.ds(pl.multiple_of(i * chunk, chunk), chunk)

    def project(which, i):
        pbuf[which, span(i), :] = jnp.dot(
            cbuf[which, span(i), :], xb[...], preferred_element_type=jnp.float32
        ).astype(jnp.bfloat16)

    def to_a(i, where):
        return send(pbuf.at[0, span(i), :], abuf.at[0, span(i), :], csend.at[0, i], crecv.at[0, i], where)

    def to_b(i, where):
        return send(pbuf.at[1, span(i), :], abuf.at[1, span(i), :], csend.at[1, i], crecv.at[1, i], where)

    def to_f(which, i, where):
        return send(
            pbuf.at[which, span(i), :], fbuf.at[span(i), :], csend.at[which, i], crecv.at[2, i], where
        )

    up1 = (lax.rem(s + 1, slots), t)

    def out_copies(section, i):
        if section in (0, 1):
            return [to_a(i, (section + 1, t)), to_b(i, (section + 1, t))]
        if section == 2:
            return [to_f(0, i, (3, t)), to_f(1, i, (0, t)), to_f(2, i, (1, t))]
        return [to_f(0, i, (2, t))]

    near = {b: (s, flip(t, b)) for b in (1, 2, 4)} if paired else {}
    if paired:
        near[5] = (s, flip(flip(t, 4), 1))
        own = 0
        held = (1, 2, 3, 5, 6, 7)
    else:
        own = REACH
        held = tuple(o for o in range(2 * REACH + 1) if o != REACH)

    def first(i):
        return pl.ds(pl.multiple_of(i * chunk, 8), part)

    def second(i):
        return pl.ds(pl.multiple_of(i * chunk + part, 8), chunk - part)

    def relay(n, i, src, dst, part, where):
        return send(
            src.at[part, :], gbuf.at[dst, part, :], gsend.at[n, i], grecv.at[n, i], where
        )

    def gather1(i):
        if paired:
            return [
                relay(0, i, fbuf, 1, span(i), near[1]),
                relay(1, i, fbuf, 2, span(i), near[2]),
                relay(2, i, fbuf, 5, span(i), near[5]),
            ]
        copies = []
        for n, o in enumerate(held):
            d = REACH - o
            copies.append(relay(n, i, fbuf, o, span(i), (s, lax.rem(t + tiles + d, tiles))))
        return copies

    def gather2(i):
        if not paired:
            return []
        return [
            relay(3, i, gbuf.at[2], 3, span(i), near[1]),
            relay(4, i, gbuf.at[2], 6, first(i), near[4]),
            relay(5, i, gbuf.at[5], 7, second(i), near[2]),
        ]

    def gather3(i):
        if not paired:
            return []
        return [
            relay(6, i, gbuf.at[6], 7, first(i), near[1]),
            relay(7, i, gbuf.at[7], 6, second(i), near[1]),
        ]

    def block_of(slot):
        if paired:
            tile = t
            for bit in (1, 2, 4):
                if slot & bit:
                    tile = flip(tile, bit)
            offset = lax.rem(tile - t + tiles + REACH, tiles) - REACH
        else:
            offset = slot - REACH
        found = jnp.int32(pairs)
        for k in range(pairs):
            found = jnp.where(off_ref[0, k] == offset, jnp.int32(k), found)
        return found

    loads[0].wait()
    loads[1].wait()
    loads[2].wait()
    loads[3].start()

    def phase_a(i, carry):
        @pl.when(s == 0)
        def _():
            project(0, i)
            to_a(i, (1, t)).start()
            project(1, i)
            to_b(i, (1, t)).start()

        @pl.when(s == 2)
        def _():
            project(2, i)
            to_f(2, i, (1, t)).start()
            project(1, i)
            to_f(1, i, (0, t)).start()

        @pl.when(s == 3)
        def _():
            project(0, i)
            to_f(0, i, (2, t)).start()

        return carry

    def send_halos(i, carry):
        for copy in halos(i):
            copy.start()
        return carry

    lax.fori_loop(0, count, send_halos, 0)
    lax.fori_loop(0, count, phase_a, 0)
    blocks = {slot: block_of(slot) for slot in (own,) + held}

    def add_to(which, landed, i):
        pbuf[which, span(i), :] = (
            pbuf[which, span(i), :].astype(jnp.float32) + landed[span(i), :].astype(jnp.float32)
        ).astype(jnp.bfloat16)

    def forcing(i):
        @pl.when(s == 1)
        def _():
            project(0, i)
            to_a(i, (2, t)).wait_recv()
            add_to(0, abuf.at[0], i)
            to_a(i, (2, t)).start()
            project(1, i)
            to_b(i, (2, t)).wait_recv()
            add_to(1, abuf.at[1], i)
            to_b(i, (2, t)).start()

        @pl.when(s == 2)
        def _():
            project(0, i)
            to_a(i, (3, t)).wait_recv()
            add_to(0, abuf.at[0], i)
            to_f(0, i, (3, t)).start()
            to_b(i, (3, t)).wait_recv()

        to_f(0, i, up1).wait_recv()

        @pl.when(s == 2)
        def _():
            fbuf[span(i), :] = (
                fbuf[span(i), :].astype(jnp.float32) + abuf[1, span(i), :].astype(jnp.float32)
            ).astype(jnp.bfloat16)

        for copy in gather1(i):
            copy.start()

    def diffuse(i):
        lane = lax.broadcasted_iota(jnp.int32, (16, columns), 1)
        inner_low = lane > 0
        inner_high = lane < columns - 1

        def block(j, carry):
            rows = pl.ds(pl.multiple_of(i * chunk + j * 16, 16), 16)
            scale = rate[rows, :]
            planes = [
                halo[0, rows, r * columns : (r + 1) * columns].astype(jnp.float32) for r in range(SWEEPS)
            ]
            planes += [x_ref[r, rows, :] for r in range(rows_here)]
            planes += [
                halo[1, rows, r * columns : (r + 1) * columns].astype(jnp.float32) for r in range(SWEEPS)
            ]
            for _ in range(SWEEPS):
                fresh = []
                for r in range(1, len(planes) - 1):
                    mid = planes[r]
                    left = jnp.where(inner_low, pltpu.roll(mid, 1, 1), 0.0)
                    right = jnp.where(inner_high, pltpu.roll(mid, columns - 1, 1), 0.0)
                    lap = planes[r + 1] + planes[r - 1] + right + left - 4.0 * mid
                    fresh.append(mid + scale * lap)
                planes = fresh
            for r in range(rows_here):
                out_ref[r, rows, :] = planes[r]
            return carry

        lax.fori_loop(0, chunk // 16, block, 0)

    def finish(i):
        dims = (((1,), (0,)), ((), ()))
        total = lax.dot_general(
            fbuf[span(i), :], wbuf[blocks[own]], dims, preferred_element_type=jnp.float32
        )
        for slot in held:
            total += lax.dot_general(
                gbuf[slot, span(i), :], wbuf[blocks[slot]], dims, preferred_element_type=jnp.float32
            )
        for r in range(rows_here):
            here = total[:, r * columns : (r + 1) * columns]
            out_ref[r, span(i), :] = jnp.where(
                mask_ref[r] == 1, out_ref[r, span(i), :] + here, x_ref[r, span(i), :]
            )

    late = jnp.where((s == 1) | (s == 2), EXTRA, 0)

    def store(i):
        return pltpu.make_async_copy(
            out_ref.at[:, span(i), :], result_ref.at[:, span(i), :], osem.at[i]
        )

    ahead = (s == 0) | (s == 3)
    per = -(-pairs // 3)

    def turn(k):
        @pl.when(k < pairs)
        def _():
            wbuf[k] = wraw[k].T

    def spread(i):
        for copy in halos(i):
            copy.wait_recv()
        diffuse(i)

    def phase_b(i, carry):
        @pl.when((i < count) & ahead)
        def _():
            spread(i)

        @pl.when(i < count)
        def _():
            forcing(i)

        @pl.when(i == 0)
        def _():
            loads[3].wait()

        @pl.when(i < 3)
        def _():
            for k in range(per):
                turn(i * per + k)

        @pl.when((i < count) & jnp.logical_not(ahead))
        def _():
            spread(i)

        j1 = i - 1 - late
        j2 = j1 - 1
        j3 = j1 - 2

        if paired:
            @pl.when((j1 >= 0) & (j1 < count))
            def _():
                one = gather1(j1)
                two = gather2(j1)
                one[1].wait_recv()
                two[0].start()
                two[1].start()
                one[2].wait_recv()
                two[2].start()

            @pl.when((j2 >= 0) & (j2 < count))
            def _():
                two = gather2(j2)
                three = gather3(j2)
                two[1].wait_recv()
                three[0].start()
                two[2].wait_recv()
                three[1].start()

        @pl.when((j3 >= 0) & (j3 < count))
        def _():
            if paired:
                gather1(j3)[0].wait_recv()
                gather2(j3)[0].wait_recv()
                for copy in gather3(j3):
                    copy.wait_recv()
            else:
                for copy in gather1(j3):
                    copy.wait_recv()
            finish(j3)
            store(j3).start()

        return carry

    lax.fori_loop(0, count + 3 + EXTRA, phase_b, 0)

    def drain(i, carry):
        for section in range(slots):
            @pl.when(s == section)
            def _():
                for copy in out_copies(section, i):
                    copy.wait_send()
        for copy in gather1(i) + gather2(i) + gather3(i) + halos(i):
            copy.wait_send()
        store(i).wait()
        return carry

    lax.fori_loop(0, count, drain, 0)


def shards(slots, tiles, coupled_state, diffusivity, coupling, regrid_weights, source_offsets, sea_mask):
    _, channels, rows_here, columns = coupled_state.shape
    cells = rows_here * columns
    pairs = regrid_weights.shape[2]
    chunk = CHUNK
    count = channels // chunk
    vmem = pl.BlockSpec(memory_space=pltpu.VMEM)
    smem = pl.BlockSpec(memory_space=pltpu.SMEM)
    anyspace = pl.BlockSpec(memory_space=pl.ANY)
    dma = pltpu.SemaphoreType.DMA
    low = jnp.bfloat16
    held = 8 if tiles == 8 else 2 * REACH + 1
    result = pl.pallas_call(
        functools.partial(body, slots, tiles, chunk),
        out_shape=jax.ShapeDtypeStruct((rows_here, channels, columns), jnp.float32),
        in_specs=[anyspace, vmem, anyspace, anyspace, smem, vmem],
        out_specs=anyspace,
        scratch_shapes=[
            pltpu.VMEM((rows_here, channels, columns), jnp.float32),
            pltpu.VMEM((rows_here, channels, columns), jnp.float32),
            pltpu.VMEM((channels, cells), low),
            pltpu.VMEM((channels, columns), jnp.float32),
            pltpu.VMEM((3, channels, channels), low),
            pltpu.VMEM((pairs, cells, cells), low),
            pltpu.VMEM((pairs + 1, cells, cells), low),
            pltpu.VMEM((held, channels, cells), low),
            pltpu.VMEM((3, channels, cells), low),
            pltpu.VMEM((2, channels, cells), low),
            pltpu.VMEM((channels, cells), low),
            pltpu.VMEM((2, channels, SWEEPS * columns), low),
            dma((3, count)),
            dma((3, count)),
            dma((2, count)),
            dma((2, count)),
            dma((8, count)),
            dma((8, count)),
            dma((5,)),
            dma((count,)),
        ],
        compiler_params=pltpu.CompilerParams(
            collective_id=0, has_side_effects=True, vmem_limit_bytes=60 * 1024 * 1024
        ),
        name="exchange",
    )(
        coupled_state[0].transpose(1, 0, 2),
        diffusivity,
        coupling[0],
        regrid_weights[0, 0],
        source_offsets[0],
        sea_mask[0][:, None, :],
    )
    return result.transpose(1, 0, 2)[None]


def solution(mesh):
    in_specs = (
        P("comp", None, "tile", None),
        P("comp", None),
        P("comp", None, None, None),
        P("comp", "tile", None, None, None),
        P("comp", "tile", None),
        P("comp", "tile", None),
    )
    out_specs = P("comp", None, "tile", None)
    run = functools.partial(shards, mesh.shape["comp"], mesh.shape["tile"])
    return jax.shard_map(run, mesh=mesh, in_specs=in_specs, out_specs=out_specs, check_vma=False)
```
